32 devices in a mesh: expert: 8 (over z, x), dp: 4 (over y, core).
Axes of the slice: x: 2, y: 2, z: 4, core: 2. Of those that a mesh axis runs over, the one named last changes fastest.
Arguments:
- tokens: bfloat16 [8192, 1024], P(('expert', 'dp')), may hold values from -6 to 6
- route_ids: int32 [8192, 2], P(('expert', 'dp')), may hold values from 0 to 7, all different within a row; in each aligned block of 256 rows (0 to 255, 256 to 511, ...) at most 96 rows name the same one
- gate_values: float32 [8192, 2], P(('expert', 'dp')), may hold values from 0.2 to 1
- w_gate: bfloat16 [8, 1024, 1024], P('expert', 'dp'), may hold values from -0.1875 to 0.1875
- w_up: bfloat16 [8, 1024, 1024], P('expert', 'dp'), may hold values from -0.1875 to 0.1875
- w_down: bfloat16 [8, 1024, 1024], P('expert', 'dp'), may hold values from -0.1875 to 0.1875
- swap_flags: int32 [8], replicated, may hold values from 0 to 1, as said below
- out_grad: bfloat16 [8192, 1024], P(('expert', 'dp')), may hold values from -6 to 6
Outputs:
- layer_out: bfloat16 [8192, 1024], P(('expert', 'dp'))
- grad_tokens: bfloat16 [8192, 1024], P(('expert', 'dp'))
- grad_gate: float32 [8, 1024, 1024], P('expert', 'dp')
- grad_up: float32 [8, 1024, 1024], P('expert', 'dp')
- grad_down: float32 [8, 1024, 1024], P('expert', 'dp')
The draws below stay inside these ranges and needn't reach their ends.
Inputs may be any that keep to these rules, and one draw needn't show every extreme that they name: `route_ids`: within the rows of one device (256 tokens) no expert is named by more than 96 token-expert pairs, a bound that some block reaches; a token's 2 experts differ. `swap_flags`: the first and the last pair always exchange their experts.
All inputs are finite; a program needn't handle non-finite values.
Results may differ from the reference program's by a relative error of at most 0.012.
Values may be sent and summed in bfloat16 or wider, within the bound.
A program may use at most 64 MiB of HBM per device.

```python
import math
import jax
import jax.numpy as jnp
import numpy as np
from jax import lax

D = 1024
F = 1024
EXP_DEV = 1
TOP = 2
TOK_DEV = 256
EXPERTS = 8
CAP = 96
TOKENS = 8192
SWAP_PAIRS = 4
N_EXPERT = 8
N_DP = 4


def draw_swap_flags(key, part):
    flag_bits = jax.random.randint(key, (N_EXPERT,), 0, 2).astype(jnp.int32)
    flag_bits = flag_bits.at[0].set(1 - flag_bits[SWAP_PAIRS])
    flag_bits = flag_bits.at[SWAP_PAIRS - 1].set(1 - flag_bits[N_EXPERT - 1])
    return flag_bits.astype(jnp.int32)


def level_of(own_key, extent, pieces, smallest, top_value):
    level, own = 1.0, jax.random.fold_in(own_key, 6)
    for axis_at, parts in pieces:
        heights = jnp.exp(jax.random.uniform(jax.random.fold_in(own, axis_at), (parts,), jnp.float32, smallest / len(pieces), top_value / len(pieces)))
        level = level * jnp.repeat(heights, extent[axis_at] // parts).reshape([-1 if axis == axis_at else 1 for axis in range(len(extent))])
    return level


def deal_out(rng, own, number, rows, count, top, most, skew):
    sequence = jax.random.permutation(rng, count)
    packed, ordinary = load_shares(count, rows * top, most, skew, True), load_shares(count, rows * top, most, skew, False)
    places = jnp.arange(count)

    def named(tallies, turn):
        used = int((tallies > 0).sum())
        fixed = max(1, used // 4)
        shifted = fixed + (places - fixed + turn * (used - fixed)) % max(1, count - fixed)
        return jnp.zeros((count,), jnp.int32).at[sequence[jnp.where(places < fixed, places, shifted)]].set(jnp.asarray(tallies, jnp.int32))

    tallies = jnp.where(number % 4 == 0, named(packed, number // 4), named(ordinary, number - number // 4 - 1))
    mixed = jax.random.permutation(jax.random.fold_in(own, 3), count)
    source_of, sink = mixed[0:count // 2 * 2:2], mixed[1:count // 2 * 2:2]
    slack = jnp.minimum(tallies[source_of] - 1, most - tallies[sink]) // 2
    slack = jnp.where((source_of == sequence[0]) | (sink == sequence[0]) | (tallies[sink] == 0), 0, jnp.maximum(slack, 0))
    shifted = jax.random.randint(jax.random.fold_in(own, 4), (count // 2,), 0, 1 << 20) % (slack + 1)
    tallies = tallies.at[source_of].add(-shifted).at[sink].add(shifted)
    items = jnp.searchsorted(jnp.cumsum(tallies), jnp.arange(rows * top), side="right").astype(jnp.int32)
    listing = items.reshape(top, rows).T
    listing = listing[jax.random.permutation(jax.random.fold_in(own, 1), rows)]
    turn = jax.random.randint(jax.random.fold_in(own, 2), (rows, 1), 0, top)
    return jnp.take_along_axis(listing, (jnp.arange(top)[None, :] + turn) % top, axis=1)


def load_shares(count, total, most, skew, full):
    portions = [(1 << 20) // math.isqrt(standing ** skew) + 1 for standing in range(1, count + 1)]
    largest = most if full else min(most, max(-(-total // count), total * portions[0] // sum(portions)))
    least = 1 if total - largest >= count - 1 else 0
    holding, rest = [largest] + [least] * (count - 1), total - largest - least * (count - 1)
    while rest > 0:
        movable = [i for i in range(1, count) if holding[i] < largest] or [i for i in range(1, count) if holding[i] < most]
        pool, budget = sum([portions[i] for i in movable]), rest
        for i in movable:
            addition = min(most - holding[i], max(1, budget * portions[i] // pool), rest)
            holding[i] = holding[i] + addition
            rest = rest - addition
    return np.array(holding)


def centred(own_key, shape, width, limit, cuts=(), kind=jnp.bfloat16):
    gain = level_of(own_key, shape, cuts, -0.22, 0.18) if cuts else 1.0
    array = jax.random.normal(own_key, shape, jnp.float32) * width * gain
    return jnp.minimum(jnp.maximum(array, -limit), limit).astype(kind)


def setup_inputs(seed: int = 0) -> dict:
    keys = jax.random.split(jax.random.key(seed), 9)
    tokens = centred(keys[0], (TOKENS, D), 1.0, 6.0, ((0, 32),))
    route_ids_keys = jax.random.split(jax.random.fold_in(keys[1], 1), TOKENS // TOK_DEV)
    route_ids_turns = jax.random.permutation(jax.random.fold_in(keys[1], 3), TOKENS // TOK_DEV)
    route_ids = jax.vmap(lambda own, number: deal_out(jax.random.fold_in(keys[1], 2), own, number, TOK_DEV, EXPERTS, TOP, CAP, 1))(route_ids_keys, route_ids_turns).reshape((TOKENS, TOP))
    gate_values = jnp.clip(0.2 + 0.8 * jax.random.uniform(keys[2], (TOKENS, TOP), jnp.float32) ** level_of(keys[2], (TOKENS, TOP), ((0, 32),), -0.2, 0.2), 0.2, 1.0)
    w_gate = centred(keys[3], (EXPERTS, D, F), D ** -0.5, 0.1875, ((0, 8), (1, 4)))
    w_up = centred(keys[4], (EXPERTS, D, F), D ** -0.5, 0.1875, ((0, 8), (1, 4)))
    w_down = centred(keys[5], (EXPERTS, F, D), F ** -0.5, 0.1875, ((0, 8), (1, 4)))
    swap_flags = draw_swap_flags(jax.random.fold_in(keys[8], 71), 0)
    out_grad = centred(keys[7], (TOKENS, D), 1.0, 6.0, ((0, 32),))
    return {"tokens": tokens, "route_ids": route_ids, "gate_values": gate_values, "w_gate": w_gate, "w_up": w_up, "w_down": w_down, "swap_flags": swap_flags, "out_grad": out_grad}


def round_half(values):
    return lax.optimization_barrier(values.astype(jnp.bfloat16)).astype(jnp.float32)


def reference(tokens, route_ids, gate_values, w_gate, w_up, w_down, swap_flags, out_grad):
    blocks = N_EXPERT * N_DP
    experts = EXP_DEV * N_EXPERT
    copies = TOK_DEV * TOP
    route_rows = route_ids.reshape(blocks, copies)
    onehot = (route_rows[:, :, None] == jnp.arange(experts, dtype=jnp.int32)[None, None, :]).astype(jnp.int32)
    rank_of = jnp.sum(jnp.cumsum(onehot, axis=1) * onehot, axis=2) - 1
    block_ids = jnp.broadcast_to(jnp.arange(blocks, dtype=jnp.int32)[:, None], (blocks, copies))
    copy_ids = jnp.broadcast_to(jnp.arange(copies, dtype=jnp.int32)[None, :], (blocks, copies))
    slot_table = jnp.full((blocks, experts, CAP), -1, jnp.int32).at[block_ids, route_rows, rank_of].set(copy_ids)
    gate_rows = gate_values.reshape(blocks, copies).astype(jnp.float32)
    column_ids = jnp.arange(blocks, dtype=jnp.int32)[:, None]

    def one_expert(totals, expert):
        mixed_sum, token_sum = totals
        rows_of = slot_table[:, expert, :]
        is_live = rows_of >= 0
        copy_pick = jnp.maximum(rows_of, 0)
        token_pick = (column_ids * TOK_DEV + copy_pick // TOP).reshape(-1)
        gate_pick = jnp.where(is_live, gate_rows[column_ids, copy_pick], 0.0).reshape(-1, 1)
        live_col = is_live.reshape(-1, 1)
        token_in = jnp.where(live_col, tokens[token_pick].astype(jnp.float32), 0.0)
        cot_in = round_half(gate_pick * out_grad[token_pick].astype(jnp.float32))
        gate_w = w_gate[expert].astype(jnp.float32)
        up_w = w_up[expert].astype(jnp.float32)
        down_w = w_down[expert].astype(jnp.float32)
        pre_gate = jnp.dot(token_in, gate_w)
        pre_up = jnp.dot(token_in, up_w)
        hidden = round_half(jax.nn.silu(pre_gate) * pre_up)
        expert_out = round_half(jnp.dot(hidden, down_w))
        mixed_sum = mixed_sum.at[token_pick].add(gate_pick * expert_out)
        grad_h = jnp.dot(cot_in, down_w.T)
        sigmoid_a = jax.nn.sigmoid(pre_gate)
        grad_a = round_half(grad_h * pre_up * sigmoid_a * (1.0 + pre_gate * (1.0 - sigmoid_a)))
        grad_b = round_half(grad_h * pre_gate * sigmoid_a)
        copy_grad = round_half(jnp.dot(grad_a, gate_w.T) + jnp.dot(grad_b, up_w.T))
        token_sum = token_sum.at[token_pick].add(copy_grad)
        token_four = token_in.reshape(N_EXPERT, N_DP, CAP, D)
        hidden_four = hidden.reshape(N_EXPERT, N_DP, CAP, F)
        cot_four = cot_in.reshape(N_EXPERT, N_DP, CAP, D)
        part_gate = round_half(jnp.einsum('idcx,idcf->dxf', token_four, grad_a.reshape(N_EXPERT, N_DP, CAP, F)))
        part_up = round_half(jnp.einsum('idcx,idcf->dxf', token_four, grad_b.reshape(N_EXPERT, N_DP, CAP, F)))
        part_down = round_half(jnp.einsum('idcf,idcx->dfx', hidden_four, cot_four))
        return (mixed_sum, token_sum), (jnp.sum(part_gate, axis=0), jnp.sum(part_up, axis=0), jnp.sum(part_down, axis=0))

    start_sums = (jnp.zeros((TOKENS, D), jnp.float32), jnp.zeros((TOKENS, D), jnp.float32))
    (mixed_sum, token_sum), stacked = lax.scan(one_expert, start_sums, jnp.arange(experts, dtype=jnp.int32))
    expert_ids = jnp.arange(experts, dtype=jnp.int32)
    owner = expert_ids // EXP_DEV
    pair_of = owner % SWAP_PAIRS
    paired = swap_flags[pair_of] != swap_flags[pair_of + SWAP_PAIRS]
    holder = jnp.where(paired, (owner + SWAP_PAIRS) % N_EXPERT, owner)
    slot_of = (holder * EXP_DEV + expert_ids % EXP_DEV).astype(jnp.int32)
    return (mixed_sum.astype(jnp.bfloat16), token_sum.astype(jnp.bfloat16), stacked[0][slot_of], stacked[1][slot_of], stacked[2][slot_of])
```

```python
import jax
import jax.numpy as jnp
from jax import lax
from jax.sharding import Mesh, PartitionSpec as P

BF = jnp.bfloat16
F32 = jnp.float32


def flip(value, axis):
    return lax.ppermute(value, axis, [(0, 1), (1, 0)])


def flip_bit(value, axis, bit):
    size = lax.axis_size(axis)
    return lax.ppermute(value, axis, [(i, i ^ (1 << bit)) for i in range(size)])


def pick_two(first, low, high):
    return jnp.where(first, low, high), jnp.where(first, high, low)


def gather_weight(shard, half, side, rest):
    other = flip(shard, "h")
    same = half == side
    keep, send = pick_two(same, shard, other)
    got = flip(send, "b")
    low, high = pick_two(side == 0, keep, got)
    rows, cols = shard.shape
    block = jnp.stack([low, high])[:, None]
    size = lax.axis_size("r")
    for bit in range(size.bit_length() - 1):
        came = flip_bit(block, "r", bit)
        upper = (rest >> bit) & 1
        first, second = pick_two(upper == 0, block, came)
        block = jnp.concatenate([first, second], axis=1)
    return block.reshape(2 * size * rows, cols)


def reduce_grad(partial, half, side, rest, paired):
    size = lax.axis_size("r")
    rows = partial.shape[0] // (2 * size)
    block = partial.reshape(2, size, rows, partial.shape[1])
    for bit in reversed(range(size.bit_length() - 1)):
        upper = (rest >> bit) & 1
        low, high = jnp.split(block, 2, axis=1)
        mine, send = pick_two(upper == 0, low, high)
        came = flip_bit(send, "r", bit)
        block = (mine.astype(F32) + came.astype(F32)).astype(BF)
    block = block[:, 0]
    mine, send = pick_two(side == 0, block[0], block[1])
    came = flip(send, "b")
    final_side = jnp.where(paired, 1 - half, half)
    keep, send = pick_two(side == final_side, mine, came)
    return keep.astype(F32) + flip(send, "h").astype(F32)


def dot(a, b, a_dim, b_dim, kind=F32):
    return lax.dot_general(a, b, (((a_dim,), (b_dim,)), ((), ())), preferred_element_type=kind)


def shards(tokens, route_ids, gate_values, w_gate, w_up, w_down, swap_flags, out_grad):
    half, l_index = lax.axis_index("h"), lax.axis_index("l")
    side, rest = lax.axis_index("b"), lax.axis_index("r")
    half_axis = lax.axis_size("l")
    experts = 2 * half_axis
    tok_rows, width = tokens.shape
    top_k = route_ids.shape[1]
    slot_cap = 3 * tok_rows * top_k // (2 * experts)
    total_slots = experts * slot_cap
    paired = jnp.take(swap_flags, l_index) != jnp.take(swap_flags, l_index + half_axis)

    full_gate = gather_weight(w_gate[0], half, side, rest)
    full_up = gather_weight(w_up[0], half, side, rest)
    full_down = gather_weight(w_down[0], half, side, rest)

    matches = [
        route_ids[:, k, None] == jnp.arange(experts, dtype=jnp.int32)[None] for k in range(top_k)
    ]
    named = sum(match.astype(BF) for match in matches)
    earlier = jnp.tril(jnp.ones((tok_rows, tok_rows), BF), -1)
    before = dot(earlier, named, 1, 0)
    slot_ids = jnp.arange(total_slots, dtype=jnp.int32)[None]
    selected = []
    for k in range(top_k):
        rank = jnp.sum(jnp.where(matches[k], before, 0.0), axis=1).astype(jnp.int32)
        selected.append((route_ids[:, k] * slot_cap + rank)[:, None] == slot_ids)
    chosen = [one.astype(BF) for one in selected]
    picks = sum(chosen)
    slot_gate = sum(
        jnp.sum(jnp.where(selected[k], gate_values[:, k, None], 0.0), axis=0) for k in range(top_k)
    )

    def exchange(rows):
        return lax.all_to_all(
            rows.reshape(experts, slot_cap, width),
            ("b", "l"),
            split_axis=0,
            concat_axis=0,
            tiled=True,
        ).reshape(total_slots, width)

    send_x = dot(picks, tokens, 0, 0, BF)
    send_c = (slot_gate[:, None] * dot(picks, out_grad, 0, 0)).astype(BF)
    recv_x = exchange(send_x)
    recv_c = exchange(send_c)

    pre_gate = dot(recv_x, full_gate, 1, 0)
    pre_up = dot(recv_x, full_up, 1, 0)
    hidden = (jax.nn.silu(pre_gate) * pre_up).astype(BF)
    dw_down = dot(hidden, recv_c, 0, 0).astype(BF)
    grad_down = reduce_grad(dw_down, half, side, rest, paired)
    grad_h = dot(recv_c, full_down, 1, 1)
    sigmoid_a = jax.nn.sigmoid(pre_gate)
    grad_a = (grad_h * pre_up * sigmoid_a * (1.0 + pre_gate * (1.0 - sigmoid_a))).astype(BF)
    grad_b = (grad_h * pre_gate * sigmoid_a).astype(BF)
    grad_gate = reduce_grad(dot(recv_x, grad_a, 0, 0).astype(BF), half, side, rest, paired)
    grad_up = reduce_grad(dot(recv_x, grad_b, 0, 0).astype(BF), half, side, rest, paired)

    expert_out = dot(hidden, full_down, 1, 0).astype(BF)
    returned_out = exchange(expert_out)
    layer_out = sum(
        gate_values[:, k, None] * dot(chosen[k], returned_out, 1, 0) for k in range(top_k)
    ).astype(BF)
    copy_grad = (dot(grad_a, full_gate, 1, 1) + dot(grad_b, full_up, 1, 1)).astype(BF)
    returned_grad = exchange(copy_grad)
    grad_tokens = dot(picks, returned_grad, 1, 0).astype(BF)
    return layer_out, grad_tokens, grad_gate[None], grad_up[None], grad_down[None]


def solution(mesh):
    n_expert, n_dp = mesh.shape["expert"], mesh.shape["dp"]
    split = Mesh(mesh.devices.reshape(2, n_expert // 2, 2, n_dp // 2), ("h", "l", "b", "r"))
    rows = P(("h", "l", "b", "r"), None)
    weight = P(("h", "l"), ("b", "r"), None)
    return jax.shard_map(
        shards,
        mesh=split,
        in_specs=(rows, rows, rows, weight, weight, weight, P(), rows),
        out_specs=(rows, rows, weight, weight, weight),
        check_vma=False,
    )
```

```python
import jax
import jax.numpy as jnp
from jax import lax
from jax.sharding import Mesh, PartitionSpec as P


BF = jnp.bfloat16
F32 = jnp.float32


def flip(value, axis):
    return lax.ppermute(value, axis, [(0, 1), (1, 0)])


def flip_bit(value, axis, bit):
    size = lax.axis_size(axis)
    return lax.ppermute(value, axis, [(i, i ^ (1 << bit)) for i in range(size)])


def pick_two(first, low, high):
    return jnp.where(first, low, high), jnp.where(first, high, low)


def gather_weight(shard, half, side, rest):
    other = flip(shard, "h")
    same = half == side
    keep, send = pick_two(same, shard, other)
    got = flip(send, "b")
    low, high = pick_two(side == 0, keep, got)
    rows, cols = shard.shape
    block = jnp.stack([low, high])[:, None]
    size = lax.axis_size("r")
    for bit in range(size.bit_length() - 1):
        came = flip_bit(block, "r", bit)
        upper = (rest >> bit) & 1
        first, second = pick_two(upper == 0, block, came)
        block = jnp.concatenate([first, second], axis=1)
    return block.reshape(2 * size * rows, cols)


def reduce_grad(partial, half, side, rest, paired):
    size = lax.axis_size("r")
    rows = partial.shape[0] // (2 * size)
    block = partial.reshape(2, size, rows, partial.shape[1])
    for bit in reversed(range(size.bit_length() - 1)):
        upper = (rest >> bit) & 1
        low, high = jnp.split(block, 2, axis=1)
        mine, send = pick_two(upper == 0, low, high)
        came = flip_bit(send, "r", bit)
        block = (mine.astype(F32) + came.astype(F32)).astype(BF)
    block = block[:, 0]
    mine, send = pick_two(side == 0, block[0], block[1])
    came = flip(send, "b")
    final_side = jnp.where(paired, 1 - half, half)
    keep, send = pick_two(side == final_side, mine, came)
    came = flip(send, "h")
    return keep.astype(F32) + came.astype(F32)


def dot(a, b, a_dim, b_dim, kind=F32):
    return lax.dot_general(a, b, (((a_dim,), (b_dim,)), ((), ())), preferred_element_type=kind)


def shards(tokens, route_ids, gate_values, w_gate, w_up, w_down, swap_flags, out_grad):
    half, l_index = lax.axis_index("h"), lax.axis_index("l")
    side, rest = lax.axis_index("b"), lax.axis_index("r")
    half_axis = lax.axis_size("l")
    experts = 2 * half_axis
    tok_rows, width = tokens.shape
    top_k = route_ids.shape[1]
    slot_cap = 3 * tok_rows * top_k // (2 * experts)
    total_slots = experts * slot_cap
    paired = jnp.take(swap_flags, l_index) != jnp.take(swap_flags, l_index + half_axis)

    full_gate = gather_weight(w_gate[0], half, side, rest)
    full_up = gather_weight(w_up[0], half, side, rest)
    full_down = gather_weight(w_down[0], half, side, rest)

    matches = [
        route_ids[:, k, None] == jnp.arange(experts, dtype=jnp.int32)[None] for k in range(top_k)
    ]
    named = sum(match.astype(BF) for match in matches)
    earlier = jnp.tril(jnp.ones((tok_rows, tok_rows), BF), -1)
    before = dot(earlier, named, 1, 0)
    slot_ids = jnp.arange(total_slots, dtype=jnp.int32)[None]
    selected = []
    for k in range(top_k):
        rank = jnp.sum(jnp.where(matches[k], before, 0.0), axis=1).astype(jnp.int32)
        selected.append((route_ids[:, k] * slot_cap + rank)[:, None] == slot_ids)
    chosen = [one.astype(BF) for one in selected]
    picks = sum(chosen)
    slot_gate = sum(
        jnp.sum(jnp.where(selected[k], gate_values[:, k, None], 0.0), axis=0) for k in range(top_k)
    )

    def exchange(rows):
        return lax.all_to_all(
            rows.reshape(experts, slot_cap, rows.shape[1]),
            ("b", "l"),
            split_axis=0,
            concat_axis=0,
            tiled=True,
        ).reshape(total_slots, rows.shape[1])

    send_x = dot(picks, tokens, 0, 0, BF)
    send_c = (slot_gate[:, None] * dot(picks, out_grad, 0, 0)).astype(BF)
    both = exchange(jnp.concatenate([send_x, send_c], axis=1))
    recv_x, recv_c = both[:, :width], both[:, width:]

    pre_gate = dot(recv_x, full_gate, 1, 0)
    pre_up = dot(recv_x, full_up, 1, 0)
    hidden = (jax.nn.silu(pre_gate) * pre_up).astype(BF)
    pre_gate, pre_up, hidden = lax.optimization_barrier((pre_gate, pre_up, hidden))
    dw_down = dot(hidden, recv_c, 0, 0).astype(BF)
    grad_down = reduce_grad(dw_down, half, side, rest, paired)
    grad_h = dot(recv_c, full_down, 1, 1)
    sigmoid_a = jax.nn.sigmoid(pre_gate)
    grad_a = (grad_h * pre_up * sigmoid_a * (1.0 + pre_gate * (1.0 - sigmoid_a))).astype(BF)
    grad_b = (grad_h * pre_gate * sigmoid_a).astype(BF)
    dw_gate = dot(recv_x, grad_a, 0, 0).astype(BF)
    grad_gate = reduce_grad(dw_gate, half, side, rest, paired)
    dw_up = dot(recv_x, grad_b, 0, 0).astype(BF)
    grad_up = reduce_grad(dw_up, half, side, rest, paired)

    expert_out = dot(hidden, full_down, 1, 0).astype(BF)
    returned_out = exchange(expert_out)
    layer_out = sum(
        gate_values[:, k, None] * dot(chosen[k], returned_out, 1, 0) for k in range(top_k)
    ).astype(BF)
    copy_grad = (dot(grad_a, full_gate, 1, 1) + dot(grad_b, full_up, 1, 1)).astype(BF)
    returned_grad = exchange(copy_grad)
    grad_tokens = dot(picks, returned_grad, 1, 0).astype(BF)
    return layer_out, grad_tokens, grad_gate[None], grad_up[None], grad_down[None]


def solution(mesh):
    n_expert, n_dp = mesh.shape["expert"], mesh.shape["dp"]
    split = Mesh(mesh.devices.reshape(2, n_expert // 2, 2, n_dp // 2), ("h", "l", "b", "r"))
    rows = P(("h", "l", "b", "r"), None)
    weight = P(("h", "l"), ("b", "r"), None)
    return jax.shard_map(
        shards,
        mesh=split,
        in_specs=(rows, rows, rows, weight, weight, weight, P(), rows),
        out_specs=(rows, rows, weight, weight, weight),
        check_vma=False,
    )
```
